256 devices in a mesh: seq: 8 (over x, y_hi), dp: 32 (over y_lo, z, core).
Axes of the slice: x: 4, y: 4 (y_hi: 2, y_lo: 2; y = y_hi * 2 + y_lo), z: 8, core: 2. Of those that a mesh axis runs over, the one named last changes fastest.
Arguments:
- frames: bfloat16 [64, 1024, 3072], P('dp', 'seq'), may hold values from -6 to 6
- proj_weight: bfloat16 [3072, 4608], P('dp'), may hold values from -0.109375 to 0.109375
- rate_weight: bfloat16 [3072, 24], replicated, may hold values from -0.109375 to 0.109375
- rate_bias: float32 [24], replicated, may hold values from -2 to 1
- init_weights: float32 [2, 24, 64, 256], replicated, may hold values from -0.75 to 0.75
- init_bias_hidden: float32 [24, 256], replicated, may hold values from -3 to 3
- init_bias_out: float32 [24, 64], replicated, may hold values from -3 to 3
- out_gain: float32 [1536], replicated, may hold values from 0.5 to 1.5
Outputs:
- ttt_output: bfloat16 [64, 1024, 1536], P('dp', 'seq')
The draws below stay inside these ranges and needn't reach their ends.
All inputs are finite; a program needn't handle non-finite values.
Results may differ from the reference program's by a relative error of at most 0.0091.
Values may be sent and summed in bfloat16 or wider, within the bound.
No kernel may reach another device: no remote copies, remote signals or barrier semaphores. Data moves between devices by JAX's collectives and lax.ppermute only.
A program may use at most 128 MiB of HBM per device.

```python
import math
import jax
import jax.numpy as jnp
from jax import lax

D = 3072
H = 24
HD = 64
HF = 256
MB = 64
SLAB = 128
HH = 1536
SEQLEN = 1024
NCLIPS = 64
N_SEQ = 8


def block_scale(stream_key, dims, split, smallest, top_value):
    level, own = 1.0, jax.random.fold_in(stream_key, 6)
    for axis_at, parts in split:
        draws = jnp.exp(jax.random.uniform(jax.random.fold_in(own, axis_at), (parts,), jnp.float32, smallest / len(split), top_value / len(split)))
        level = level * jnp.repeat(draws, dims[axis_at] // parts).reshape([-1 if axis == axis_at else 1 for axis in range(len(dims))])
    return level


def noise(own_key, shape, spread, reach, shards=(), kind=jnp.bfloat16):
    level = block_scale(own_key, shape, shards, -0.22, 0.18) if shards else 1.0
    values = jax.random.normal(own_key, shape, jnp.float32) * spread * level
    return jnp.minimum(jnp.maximum(values, -reach), reach).astype(kind)


def setup_inputs(seed: int = 0) -> dict:
    arg_keys = jax.random.split(jax.random.key(seed), 9)
    return {
        "frames": noise(arg_keys[0], (NCLIPS, SEQLEN, D), 1.0, 6.0, ((0, 32), (1, 8))),
        "proj_weight": noise(arg_keys[1], (D, 3 * HH), D ** -0.5, 0.109375, ((0, 32),)),
        "rate_weight": noise(arg_keys[2], (D, H), D ** -0.5, 0.109375),
        "rate_bias": jnp.clip(jax.random.uniform(arg_keys[3], (H,), jnp.float32, -2.0, 1.0), -2.0, 1.0),
        "init_weights": noise(arg_keys[4], (2, H, HD, HF), HD ** -0.5, 0.75, (), jnp.float32),
        "init_bias_hidden": noise(arg_keys[5], (H, HF), 0.5, 3.0, (), jnp.float32),
        "init_bias_out": noise(arg_keys[6], (H, HD), 0.5, 3.0, (), jnp.float32),
        "out_gain": jnp.clip(1.0 + 0.1 * jax.random.normal(arg_keys[7], (HH,), jnp.float32), 0.5, 1.5),
    }


precise = lax.Precision.HIGHEST
coefficient = 0.044715
root_scale = math.sqrt(2.0 / math.pi)

def gelu_pair(z_value):
    tanh_part = jnp.tanh(root_scale * (z_value + coefficient * z_value * z_value * z_value))
    result = 0.5 * z_value * (1.0 + tanh_part)
    derivative = 0.5 * (1.0 + tanh_part) + 0.5 * z_value * (1.0 - tanh_part * tanh_part) * root_scale * (1.0 + 3.0 * coefficient * z_value * z_value)
    return (result, derivative)

def minibatch(carried, inputs):
    pair, bias_hidden, bias_out = carried
    queries, key_rows, values, step_rate = inputs
    w_first = pair[0]
    w_second = pair[1]
    block_len = queries.shape[1]
    causal = jnp.tril(jnp.ones((block_len, block_len), dtype=bool))
    z_first = jnp.einsum('hbd,hdf->hbf', key_rows, w_first, precision=precise) + bias_hidden[:, None, :]
    hidden, derivative = gelu_pair(z_first)
    z_second = jnp.einsum('hbf,hdf->hbd', hidden, w_second, precision=precise) + bias_out[:, None, :]
    grad_second = z_second - (values - key_rows)
    grad_first = jnp.einsum('hbd,hdf->hbf', grad_second, w_second, precision=precise) * derivative
    scores_first = jnp.einsum('htd,hsd->hts', queries, key_rows, precision=precise) + 1.0
    mix_first = jnp.where(causal[None], scores_first * step_rate[:, None, :], 0.0)
    zq_first = jnp.einsum('htd,hdf->htf', queries, w_first, precision=precise) + bias_hidden[:, None, :]
    zq_first = zq_first - jnp.einsum('hts,hsf->htf', mix_first, grad_first, precision=precise)
    hidden_query, unused = gelu_pair(zq_first)
    scores_second = jnp.einsum('htf,hsf->hts', hidden_query, hidden, precision=precise) + 1.0
    mix_second = jnp.where(causal[None], scores_second * step_rate[:, None, :], 0.0)
    zq_second = jnp.einsum('htf,hdf->htd', hidden_query, w_second, precision=precise) + bias_out[:, None, :]
    zq_second = zq_second - jnp.einsum('hts,hsd->htd', mix_second, grad_second, precision=precise)
    scaled_first = grad_first * step_rate[:, :, None]
    scaled_second = grad_second * step_rate[:, :, None]
    new_first = w_first - jnp.einsum('hbd,hbf->hdf', key_rows, scaled_first, precision=precise)
    new_second = w_second - jnp.einsum('hbd,hbf->hdf', scaled_second, hidden, precision=precise)
    new_pair = jnp.stack([new_first, new_second])
    new_hidden = bias_hidden - lax.optimization_barrier(jnp.sum(scaled_first, axis=1))
    new_out = bias_out - lax.optimization_barrier(jnp.sum(scaled_second, axis=1))
    return ((new_pair, new_hidden, new_out), queries + zq_second)

def one_slab(carried, slab_inputs):
    final_state, results = lax.scan(minibatch, carried, slab_inputs)
    final_state = jax.tree.map(lambda member: lax.optimization_barrier(member.astype(jnp.bfloat16)).astype(jnp.float32), final_state)
    return (final_state, results)

def reference(frames, proj_weight, rate_weight, rate_bias, init_weights, init_bias_hidden, init_bias_out, out_gain):
    gain_rows = out_gain.reshape(H, HD)
    batches = SLAB // MB

    def one_clip(clip_frames):
        projected = jnp.dot(clip_frames, proj_weight, preferred_element_type=jnp.float32).astype(jnp.bfloat16)
        projected = projected.reshape(SEQLEN, 3, H, HD)
        rates = jax.nn.sigmoid(jnp.dot(clip_frames, rate_weight, preferred_element_type=jnp.float32) + rate_bias) / (MB * (HD + HF))
        inputs = projected.astype(jnp.float32).reshape(N_SEQ, batches, MB, 3, H, HD).transpose(3, 0, 1, 4, 2, 5)
        step_rate = rates.reshape(N_SEQ, batches, MB, H).transpose(0, 1, 3, 2)
        start_state = (init_weights, init_bias_hidden, init_bias_out)
        unused, results = lax.scan(one_slab, start_state, (inputs[0], inputs[1], inputs[2], step_rate))
        results = results.transpose(0, 1, 3, 2, 4).reshape(SEQLEN, H, HD)
        normed = results * lax.rsqrt(lax.optimization_barrier(jnp.mean(results * results, axis=-1, keepdims=True)) + 1e-06) * gain_rows
        return normed.reshape(SEQLEN, H * HD).astype(jnp.bfloat16)
    return lax.map(one_clip, frames)
```

```python
import math

import jax
import jax.numpy as jnp
from jax import lax
from jax.experimental import pallas as pl
from jax.experimental.pallas import tpu as pltpu
from jax.sharding import Mesh
from jax.sharding import PartitionSpec as P

MB = 64
PAIRS = 3
cubic = 0.044715
root_scale = math.sqrt(2.0 / math.pi)
bf16 = jnp.bfloat16
f32 = jnp.float32


def mm(a, b):
    return lax.dot_general(a, b, (((1,), (0,)), ((), ())), preferred_element_type=f32)


def mm_nt(a, b):
    return lax.dot_general(a, b, (((1,), (1,)), ((), ())), preferred_element_type=f32)


def mm_tn(a, b):
    return lax.dot_general(a, b, (((0,), (0,)), ((), ())), preferred_element_type=f32)


def gate(z):
    return 0.5 + 0.5 * jnp.tanh(z * (root_scale + (root_scale * cubic) * (z * z)))


def ttt_kernel(order_ref, proj_ref, rate_ref, w1i, w2i, b1i, b2i, gain_ref, out_ref,
               w1s, w2s, b1s, b2s):
    slab = pl.program_id(0)

    @pl.when(slab == 0)
    def _():
        w1s[...] = w1i[...]
        w2s[...] = w2i[...]
        b1s[...] = b1i[...]
        b2s[...] = b2i[...]

    row = lax.broadcasted_iota(jnp.int32, (128, 128), 0)
    col = lax.broadcasted_iota(jnp.int32, (128, 128), 1)
    same = (row // 64) == (col // 64)
    causal = same & (row >= col)
    low = lax.broadcasted_iota(jnp.int32, (64, 128), 1) < 64

    def two(x):
        zero = jnp.zeros_like(x)
        return jnp.concatenate([jnp.where(low, x, zero), jnp.where(low, zero, x)], axis=0)

    for m in range(2):
        rows = pl.ds(m * MB, MB)
        st = []
        for p in range(PAIRS):
            def part(c):
                cols = pl.ds(c * 384 + p * 128, 128)
                return proj_ref[rows, cols]
            q, k, v = part(0).astype(f32), part(1).astype(f32), part(2).astype(f32)
            qm = two(q)
            km = two(k)
            kmb = km.astype(bf16)
            qmb = qm.astype(bf16)
            target = b2s[p] - (v - k)
            rate = jnp.concatenate(
                [jnp.where(low, rate_ref[rows, 2 * p : 2 * p + 1], 0.0),
                 jnp.where(low, 0.0, rate_ref[rows, 2 * p + 1 : 2 * p + 2])], axis=0)
            w1 = w1s[p].astype(bf16)
            w2 = w2s[p].astype(bf16)
            b1 = b1s[p]
            bias = jnp.concatenate([jnp.broadcast_to(b1[0:1], (64, 256)), jnp.broadcast_to(b1[1:2], (64, 256))], axis=0)
            z1 = mm(kmb, w1) + bias
            zq = mm(qmb, w1) + bias
            st.append((qm, qmb, kmb, target, rate, w2, z1, zq))
        st2 = []
        for p in range(PAIRS):
            qm, qmb, kmb, target, rate, w2, z1, zq = st[p]
            s = gate(z1)
            x2 = (z1 * s).astype(bf16)
            slope = s + (z1 * (s - s * s)) * (2.0 * root_scale + (6.0 * root_scale * cubic) * (z1 * z1))
            z2 = mm_nt(x2, w2)
            h2 = (z2 + jnp.concatenate([target, target], axis=0)) * rate
            h2b = h2.astype(bf16)
            h1 = mm(h2b, w2) * slope
            h1b = h1.astype(bf16)
            st2.append((x2, h2, h2b, h1, h1b))
        for p in range(PAIRS):
            qm, qmb, kmb, target, rate, w2, z1, zq = st[p]
            x2, h2, h2b, h1, h1b = st2[p]
            w1n = w1s[p] - mm_tn(kmb, h1b)
            w2n = w2s[p] - mm_tn(h2b, x2)
            b1n = b1s[p] - jnp.concatenate(
                [jnp.sum(h1[:64], axis=0, keepdims=True), jnp.sum(h1[64:], axis=0, keepdims=True)], axis=0)
            b2o = b2s[p]
            b2n = b2o - jnp.sum(h2, axis=0, keepdims=True)
            if m == 1:
                w1n, w2n, b1n, b2n = [t.astype(bf16).astype(f32) for t in (w1n, w2n, b1n, b2n)]
            w1s[p] = w1n
            w2s[p] = w2n
            b1s[p] = b1n
            b2s[p] = b2n
            m1 = jnp.where(causal, mm_nt(qmb, kmb) + 1.0, 0.0).astype(bf16)
            zq = zq - mm(m1, h1b)
            xq = (zq * gate(zq)).astype(bf16)
            both = mm_nt(xq, jnp.concatenate([w2, x2], axis=0))
            m2 = jnp.where(causal, both[:, 128:] + 1.0, 0.0).astype(bf16)
            y = qm + jnp.where(same, both[:, :128] + b2o, 0.0) - mm(m2, h2b)
            y = y * lax.rsqrt(jnp.sum(y * y, axis=1, keepdims=True) * (1.0 / 64.0) + 1e-6)
            y = (y[:64] + y[64:]) * gain_ref[0:1, p * 128 : (p + 1) * 128]
            out_ref[0, rows, p * 128 : (p + 1) * 128] = y.astype(bf16)


def ttt(order, projected, rates, w1, w2, b1, b2, gain):
    def whole(shape):
        return pl.BlockSpec(shape, lambda i, order: (0,) * len(shape))

    return pl.pallas_call(
        ttt_kernel,
        out_shape=jax.ShapeDtypeStruct((8, 128, 384), bf16),
        grid_spec=pltpu.PrefetchScalarGridSpec(
            num_scalar_prefetch=1,
            grid=(8,),
            in_specs=[
                pl.BlockSpec((128, 1152), lambda i, order: (order[i], 0)),
                pl.BlockSpec((128, 6), lambda i, order: (order[i], 0)),
                whole((PAIRS, 128, 256)),
                whole((PAIRS, 128, 256)),
                whole((PAIRS, 2, 256)),
                whole((PAIRS, 1, 128)),
                whole((1, 384)),
            ],
            out_specs=pl.BlockSpec((1, 128, 384), lambda i, order: (i, 0, 0)),
            scratch_shapes=[
                pltpu.VMEM((PAIRS, 128, 256), f32),
                pltpu.VMEM((PAIRS, 128, 256), f32),
                pltpu.VMEM((PAIRS, 2, 256), f32),
                pltpu.VMEM((PAIRS, 1, 128), f32),
            ],
        ),
        compiler_params=pltpu.CompilerParams(dimension_semantics=("arbitrary",)),
        name="ttt",
    )(order, projected, rates, w1, w2, b1, b2, gain)


DP = ("yl", "z", "c")
SEQ = ("x", "yh")
swap = [(0, 1), (1, 0)]
x_up = [(i, (i + 1) % 4) for i in range(4)]
x_down = [(i, (i - 1) % 4) for i in range(4)]


def x_ring(block):
    half = block.shape[0] // 2
    below = lax.ppermute(block, "x", x_up)
    above = lax.ppermute(block, "x", x_down)
    first = lax.ppermute(below[:half], "x", x_up)
    second = lax.ppermute(above[half:], "x", x_down)
    return [block, below, above, first, second]


def on_device(
    frames,
    proj_weight,
    rate_weight,
    rate_bias,
    init_weights,
    init_bias_hidden,
    init_bias_out,
    out_gain,
):
    x = lax.axis_index("x")
    yh = lax.axis_index("yh")
    mine = lax.dynamic_index_in_dim(frames, yh, 0, keepdims=False)
    sent = lax.dynamic_index_in_dim(frames, 1 - yh, 0, keepdims=False)
    weight = lax.dynamic_slice(proj_weight.reshape(96, 3, 1536), (0, 0, x * 384), (96, 3, 384))
    weight = lax.all_gather(weight.reshape(96, 1152), DP, axis=0, tiled=True)
    theirs = lax.ppermute(sent, "yh", swap)
    tokens = jnp.concatenate(x_ring(mine) + x_ring(theirs), axis=0)
    rate_columns = lax.dynamic_slice(rate_weight, (0, x * 6), (3072, 6))
    rate_offset = lax.dynamic_slice(rate_bias, (x * 6,), (6,))
    rates = jax.nn.sigmoid(
        jnp.dot(tokens, rate_columns, preferred_element_type=f32) + rate_offset
    ) * (1.0 / 20480.0)
    projected = jnp.dot(tokens, weight, preferred_element_type=f32).astype(bf16)
    slabs = jnp.arange(8, dtype=jnp.int32)
    away = (slabs // 2 - x) % 4
    order = jnp.where(away == 0, 0, jnp.where(away == 3, 1, away + 1)) + 4 * (slabs % 2 != yh)
    pair_weights = lax.dynamic_slice(init_weights, (0, x * 6, 0, 0), (2, 6, 64, 256))
    pair_weights = pair_weights.reshape(2, PAIRS, 128, 256)
    hidden_bias = lax.dynamic_slice(init_bias_hidden, (x * 6, 0), (6, 256)).reshape(PAIRS, 2, 256)
    out_bias = lax.dynamic_slice(init_bias_out, (x * 6, 0), (6, 64)).reshape(PAIRS, 1, 128)
    gain = lax.dynamic_slice(out_gain, (x * 384,), (384,)).reshape(1, 384)
    result = ttt(
        order.astype(jnp.int32),
        projected,
        rates,
        pair_weights[0],
        pair_weights[1],
        hidden_bias,
        out_bias,
        gain,
    )
    result = lax.all_to_all(result, SEQ, 0, 0, tiled=True)
    return result.reshape(4, 2, 128, 384).transpose(1, 2, 0, 3).reshape(2, 128, 1536)


def solution(mesh):
    fine = Mesh(mesh.devices.reshape(4, 2, 2, 8, 2), ("x", "yh", "yl", "z", "c"))
    return jax.shard_map(
        on_device,
        mesh=fine,
        in_specs=(P(DP, SEQ, None), P(DP, None), P(), P(), P(), P(), P(), P()),
        out_specs=P(DP, SEQ, None),
        check_vma=False,
    )
```

```python
import math

import jax
import jax.numpy as jnp
import numpy as np
from jax import lax
from jax.experimental import pallas as pl
from jax.experimental.pallas import tpu as pltpu
from jax.sharding import Mesh
from jax.sharding import PartitionSpec as P

MB = 64
PAIRS = 3
cubic = 0.044715
root_scale = math.sqrt(2.0 / math.pi)
bf16 = jnp.bfloat16
f32 = jnp.float32


def mm(a, b):
    return lax.dot_general(a, b, (((1,), (0,)), ((), ())), preferred_element_type=f32)


def mm_nt(a, b):
    return lax.dot_general(a, b, (((1,), (1,)), ((), ())), preferred_element_type=f32)


def mm_tn(a, b):
    return lax.dot_general(a, b, (((0,), (0,)), ((), ())), preferred_element_type=f32)


def gate(z):
    return 0.5 + 0.5 * jnp.tanh(z * (root_scale + (root_scale * cubic) * (z * z)))


TOKEN_PIECES = [
    (0, 0, 128), (1, 0, 128), (2, 0, 128), (3, 0, 64), (4, 0, 64),
    (5, 0, 128), (3, 64, 128), (4, 64, 128), (6, 0, 64), (7, 0, 64),
]
NT = 8
WEIGHT_PIECES = [(h, i * 96, 96) for h in (0, 2) for i in range(14)] + [
    (h, i * 96, 96) for h in (1, 3) for i in range(2)
]


def layer_kernel(offset_ref, *refs):
    token_refs = refs[:NT]
    weight_refs = refs[NT : NT + 4]
    rwt_ref, rbias_ref, w1i, w2i, b1i, b2i, gain_ref, out_ref = refs[NT + 4 : NT + 12]
    (w1s, w2s, b1s, b2s, qm_s, wh_s, wx_s, h2_s, b1_s, b2_s, q_s,
     tokens_s, weight_s, proj_s, rate_s, sems) = refs[NT + 12 :]
    slab = pl.program_id(0)

    @pl.when(slab == 0)
    def _():
        copies = []
        for i, (ref, start, size) in enumerate(WEIGHT_PIECES):
            at = pl.multiple_of(offset_ref[len(TOKEN_PIECES) + i], 32)
            copies.append(
                pltpu.make_async_copy(
                    weight_refs[ref].at[pl.ds(start, size)], weight_s.at[pl.ds(at, size)], sems.at[i]
                )
            )
        for i, (ref, start, size) in enumerate(TOKEN_PIECES):
            at = pl.multiple_of(offset_ref[i], 64)
            copies.append(
                pltpu.make_async_copy(
                    token_refs[ref].at[pl.ds(start, size)],
                    tokens_s.at[pl.ds(at, size)],
                    sems.at[len(WEIGHT_PIECES) + i],
                )
            )
        for copy in copies:
            copy.start()
        w1s[...] = w1i[...]
        w2s[...] = w2i[...]
        b1s[...] = b1i[...]
        b2s[...] = b2i[...]
        for copy in copies:
            copy.wait()

        def project(i, carry):
            rows = pl.ds(pl.multiple_of(i * 256, 256), 256)
            for n in range(5):
                cols = pl.ds(n * 256, 256 if n < 4 else 128)
                proj_s[rows, cols] = mm(tokens_s[rows, :], weight_s[:, cols]).astype(bf16)
            logits = mm(tokens_s[rows, :], rwt_ref[...]) + rbias_ref[...]
            rate_s[rows] = (1.0 / 20480.0) / (1.0 + jnp.exp(-logits))
            return carry

        lax.fori_loop(0, 4, project, 0)

    low = lax.broadcasted_iota(jnp.int32, (64, 128), 1) < 64

    def two(x):
        zero = jnp.zeros_like(x)
        return jnp.concatenate([jnp.where(low, x, zero), jnp.where(low, zero, x)], axis=0)

    tri = lax.broadcasted_iota(jnp.int32, (64, 128), 0) >= lax.broadcasted_iota(jnp.int32, (64, 128), 1) % 64

    def one(x):
        return jnp.where(low, x[:64], x[64:])

    def train(m):
        rows = pl.ds(pl.multiple_of(slab * 128 + m * MB, MB), MB)
        D = []
        for p in range(PAIRS):
            def part(c):
                return proj_s[rows, pl.ds(c * 384 + p * 128, 128)]
            q, k, v = part(0), part(1), part(2)
            kf = k.astype(f32)
            kmb = two(k)
            w1 = w1s[p].astype(bf16); w2 = w2s[p].astype(bf16)
            b1 = b1s[p]
            bias = jnp.concatenate([jnp.broadcast_to(b1[0:1], (64, 256)), jnp.broadcast_to(b1[1:2], (64, 256))], axis=0)
            z1 = mm(kmb, w1) + bias
            D.append(dict(w1=w1, w2=w2, kmb=kmb, q=q, vk=v.astype(f32) - kf, z1=z1, b1=b1, b2=b2s[p]))
        yield
        for p in range(PAIRS):
            d = D[p]
            z1 = d["z1"]
            s = gate(z1)
            d["x2"] = (z1 * s).astype(bf16)
            d["z2"] = mm_nt(d["x2"], d["w2"])
            d["slope"] = s + (z1 * (s - s * s)) * (2.0 * root_scale + (6.0 * root_scale * cubic) * (z1 * z1))
        yield
        for p in range(PAIRS):
            d = D[p]
            rate = jnp.where(low, rate_s[rows, 2 * p : 2 * p + 1], rate_s[rows, 2 * p + 1 : 2 * p + 2])
            h2 = (one(d["z2"]) + (d["b2"] - d["vk"])) * rate
            d["h2b"] = two(h2.astype(bf16))
            d["g1"] = mm(d["h2b"], d["w2"])
            b2n = d["b2"] - jnp.sum(h2, axis=0, keepdims=True)
            if m == 1:
                b2n = b2n.astype(bf16).astype(f32)
            b2s[p] = b2n
        for p in range(PAIRS):
            d = D[p]
            d["m1"] = two(jnp.where(tri, -1.0 - mm_nt(d["q"], d["kmb"]), 0.0).astype(bf16))
            w2n = w2s[p] - mm_tn(d["h2b"], d["x2"])
            if m == 1:
                w2n = w2n.astype(bf16).astype(f32)
            w2s[p] = w2n
        yield
        for p in range(PAIRS):
            d = D[p]
            h1 = d["g1"] * d["slope"]
            h1b = h1.astype(bf16)
            w1n = w1s[p] - mm_tn(d["kmb"], h1b)
            db = jnp.concatenate([jnp.sum(h1[:64], axis=0, keepdims=True), jnp.sum(h1[64:], axis=0, keepdims=True)], axis=0)
            b1n = d["b1"] - db
            if m == 1:
                w1n = w1n.astype(bf16).astype(f32); b1n = b1n.astype(bf16).astype(f32)
            w1s[p] = w1n; b1s[p] = b1n
            d["h1b"] = h1b
        yield
        for p in range(PAIRS):
            d = D[p]
            qm_s[m, p, :, :128] = two(d["q"])
            qm_s[m, p, :, 128:] = d["m1"]
            wh_s[m, p, :128] = d["w1"]
            wh_s[m, p, 128:] = d["h1b"]
            wx_s[m, p, :128] = d["w2"]
            wx_s[m, p, 128:] = d["x2"]
            h2_s[m, p] = d["h2b"]
            b1_s[m, p] = d["b1"]
            b2_s[m, p] = d["b2"]
            q_s[m, p] = d["q"]
        yield

    def query(m, start):
        D = [dict() for _ in range(PAIRS)]
        for p in range(PAIRS):
            b1 = b1_s[m, p]
            bias = jnp.concatenate([jnp.broadcast_to(b1[0:1], (64, 256)), jnp.broadcast_to(b1[1:2], (64, 256))], axis=0)
            D[p]["zq"] = mm(qm_s[m, p], wh_s[m, p]) + bias
        yield
        for p in range(PAIRS):
            d = D[p]
            zq = d["zq"]
            xq = (zq * gate(zq)).astype(bf16)
            both = mm_nt(xq, wx_s[m, p])
            d["bw"] = both[:, :128]
            d["bx"] = both[:, 128:]
        yield
        for p in range(PAIRS):
            d = D[p]
            m2 = jnp.where(tri, one(d["bx"]) + 1.0, 0.0).astype(bf16)
            d["mh"] = mm(m2, h2_s[m, p])
        yield
        for p in range(PAIRS):
            d = D[p]
            y = q_s[m, p].astype(f32) + (one(d["bw"]) + b2_s[m, p]) - d["mh"]
            yy = y * y
            lo = jnp.sum(jnp.where(low, yy, 0.0), axis=1, keepdims=True)
            hi = jnp.sum(jnp.where(low, 0.0, yy), axis=1, keepdims=True)
            y = y * lax.rsqrt(jnp.where(low, lo, hi) * (1.0 / 64.0) + 1e-6)
            y = y * gain_ref[0:1, p * 128 : (p + 1) * 128]
            out_ref[pl.ds(start, MB), p * 128 : (p + 1) * 128] = y.astype(bf16)
        yield

    def weave(*gens):
        gens = list(gens)
        while gens:
            for g in list(gens):
                if next(g, "end") == "end":
                    gens.remove(g)

    before = pl.multiple_of(jnp.maximum(slab * 128 - MB, 0), MB)
    weave(train(0), query(1, before))
    weave(train(1), query(0, pl.multiple_of(slab * 128, MB)))

    @pl.when(slab == 7)
    def _():
        weave(query(1, pl.multiple_of(slab * 128 + MB, MB)))


def layer(offsets, tokens, weights, rwt, rbias, w1, w2, b1, b2, gain):
    def whole(shape):
        return pl.BlockSpec(shape, lambda i, offsets: (0,) * len(shape))

    anywhere = pl.BlockSpec(memory_space=pl.ANY)
    pieces = len(TOKEN_PIECES) + len(WEIGHT_PIECES)
    return pl.pallas_call(
        layer_kernel,
        out_shape=jax.ShapeDtypeStruct((1024, 384), bf16),
        grid_spec=pltpu.PrefetchScalarGridSpec(
            num_scalar_prefetch=1,
            grid=(8,),
            in_specs=[anywhere] * (NT + 4)
            + [
                whole((3072, 128)),
                whole((1, 128)),
                whole((PAIRS, 128, 256)),
                whole((PAIRS, 128, 256)),
                whole((PAIRS, 2, 256)),
                whole((PAIRS, 1, 128)),
                whole((1, 384)),
            ],
            out_specs=whole((1024, 384)),
            scratch_shapes=[
                pltpu.VMEM((PAIRS, 128, 256), f32),
                pltpu.VMEM((PAIRS, 128, 256), f32),
                pltpu.VMEM((PAIRS, 2, 256), f32),
                pltpu.VMEM((PAIRS, 1, 128), f32),
                pltpu.VMEM((2, PAIRS, 128, 256), bf16),
                pltpu.VMEM((2, PAIRS, 256, 256), bf16),
                pltpu.VMEM((2, PAIRS, 256, 256), bf16),
                pltpu.VMEM((2, PAIRS, 128, 128), bf16),
                pltpu.VMEM((2, PAIRS, 2, 256), f32),
                pltpu.VMEM((2, PAIRS, 1, 128), f32),
                pltpu.VMEM((2, PAIRS, 64, 128), bf16),
                pltpu.VMEM((1024, 3072), bf16),
                pltpu.VMEM((3072, 1152), bf16),
                pltpu.VMEM((1024, 1152), bf16),
                pltpu.VMEM((1024, 128), f32),
                pltpu.SemaphoreType.DMA((pieces,)),
            ],
        ),
        compiler_params=pltpu.CompilerParams(
            dimension_semantics=("arbitrary",), vmem_limit_bytes=32 << 20
        ),
        name="layer",
    )(offsets, *tokens, *weights, rwt, rbias, w1, w2, b1, b2, gain)


DP = ("yl", "z", "c")
SEQ = ("x", "yh")
swap = [(0, 1), (1, 0)]


def ring(size, step):
    return [(i, (i + step) % size) for i in range(size)]


def after(value, others):
    return lax.optimization_barrier((value, others))[0]


def on_device(
    frames,
    proj_weight,
    rate_weight,
    rate_bias,
    init_weights,
    init_bias_hidden,
    init_bias_out,
    out_gain,
):
    x, yh, yl, z, c = (lax.axis_index(name) for name in ("x", "yh", "yl", "z", "c"))

    mine = lax.dynamic_index_in_dim(frames, yh, 0, keepdims=False)
    sent = lax.dynamic_index_in_dim(frames, 1 - yh, 0, keepdims=False)
    theirs = lax.ppermute(sent, "yh", swap)
    below = lax.ppermute(mine, "x", ring(4, 1))
    above = lax.ppermute(mine, "x", ring(4, -1))
    below2 = lax.ppermute(jnp.concatenate([below[:64], theirs]), "x", ring(4, 1))
    above2 = lax.ppermute(jnp.concatenate([above[64:], theirs]), "x", ring(4, -1))
    below3 = lax.ppermute(below2[64:128], "x", ring(4, 1))
    above3 = lax.ppermute(above2[128:], "x", ring(4, -1))
    tokens = [mine, below, above, below2, above2, theirs, below3, above3]

    part = jnp.concatenate(
        [lax.dynamic_slice(proj_weight, (0, i * 1536 + x * 384), (96, 384)) for i in range(3)], axis=1
    )
    up = down = jnp.concatenate([part, lax.ppermute(part, "yl", swap)])
    blocks = [up]
    for step in range(3):
        if step == 1:
            up, down = after((up, down), (below, above, theirs))
        up = lax.ppermute(up, "z", ring(8, 1))
        down = lax.ppermute(down, "z", ring(8, -1))
        blocks += [up, down]
    near = jnp.concatenate(blocks)
    up, down, near = after((up, down, near), (below2, above2))
    up = lax.ppermute(up[:96], "z", ring(8, 1))
    down = lax.ppermute(down[96:], "z", ring(8, -1))
    far = jnp.concatenate([up, down])
    weights = [near, far, lax.ppermute(near, "c", swap), lax.ppermute(far, "c", swap)]

    dx = np.tile(np.array([0, -1, 1, 2, 2]), 2)
    other_slab = np.repeat([0, 1], 5)
    late_half = np.tile(np.array([0, 0, 0, 0, 64]), 2)
    slab = (x + dx) % 4 * 2 + (yh + other_slab) % 2
    dz = np.concatenate([np.tile(np.repeat([0, -1, 1, -2, 2, -3, 3], 2), 2), np.full(4, 4)])
    other_row = np.tile(np.array([0, 1]), 16)
    other_core = np.concatenate([np.repeat([0, 1], 14), np.repeat([0, 1], 2)])
    block = ((yl + other_row) % 2 * 8 + (z + dz) % 8) * 2 + (c + other_core) % 2
    offsets = jnp.concatenate([slab * 128 + late_half, block * 96]).astype(jnp.int32)

    rate_columns = jnp.pad(lax.dynamic_slice(rate_weight, (0, x * 6), (3072, 6)), ((0, 0), (0, 122)))
    rate_offset = jnp.pad(lax.dynamic_slice(rate_bias, (x * 6,), (6,)), (0, 122)).reshape(1, 128)
    pair_weights = lax.dynamic_slice(init_weights, (0, x * 6, 0, 0), (2, 6, 64, 256))
    pair_weights = pair_weights.reshape(2, PAIRS, 128, 256)
    hidden_bias = lax.dynamic_slice(init_bias_hidden, (x * 6, 0), (6, 256)).reshape(PAIRS, 2, 256)
    out_bias = lax.dynamic_slice(init_bias_out, (x * 6, 0), (6, 64)).reshape(PAIRS, 1, 128)
    gain = lax.dynamic_slice(out_gain, (x * 384,), (384,)).reshape(1, 384)
    result = layer(
        offsets, tokens, weights, rate_columns, rate_offset,
        pair_weights[0], pair_weights[1], hidden_bias, out_bias, gain,
    )
    result = lax.all_to_all(result.reshape(8, 128, 384), SEQ, 0, 0, tiled=True)
    return result.reshape(4, 2, 128, 384).transpose(1, 2, 0, 3).reshape(2, 128, 1536)


def solution(mesh):
    fine = Mesh(mesh.devices.reshape(4, 2, 2, 8, 2), ("x", "yh", "yl", "z", "c"))
    return jax.shard_map(
        on_device,
        mesh=fine,
        in_specs=(P(DP, SEQ, None), P(DP, None), P(), P(), P(), P(), P(), P()),
        out_specs=P(DP, SEQ, None),
        check_vma=False,
    )
```

```python
import math

import jax
import jax.numpy as jnp
from jax import lax
from jax.experimental import pallas as pl
from jax.experimental.pallas import tpu as pltpu
from jax.sharding import Mesh
from jax.sharding import PartitionSpec as P

MB = 64
PAIRS = 3
cubic = 0.044715
root_scale = math.sqrt(2.0 / math.pi)
bf16 = jnp.bfloat16
f32 = jnp.float32


def mm(a, b):
    return lax.dot_general(a, b, (((1,), (0,)), ((), ())), preferred_element_type=f32)


def mm_nt(a, b):
    return lax.dot_general(a, b, (((1,), (1,)), ((), ())), preferred_element_type=f32)


def mm_tn(a, b):
    return lax.dot_general(a, b, (((0,), (0,)), ((), ())), preferred_element_type=f32)


def gate(z):
    return 0.5 + 0.5 * jnp.tanh(z * (root_scale + (root_scale * cubic) * (z * z)))


NT = 10
NW = 2
TOKEN_PIECES = [
    (i, j * 64, 64) for i, count in enumerate((2, 2, 2, 2, 2, 2, 1, 1, 1, 1)) for j in range(count)
]
WEIGHT_PIECES = [(h, i * 96, 96) for h in range(NW) for i in range(16)]


def layer_kernel(place_ref, *refs):
    token_refs = refs[:NT]
    weight_refs = refs[NT : NT + NW]
    rate_t_ref, rate_bias_ref, init_ref, hidden_ref, outer_ref, gain_ref, out_ref = refs[NT + NW : NT + NW + 7]
    (w1s, w2s, b1s, b2s, qm_s, wh_s, wx_s, h2_s, b1_s, b2_s, q_s,
     tokens_s, weight_s, proj_s, rate_s, sems) = refs[NT + NW + 7 :]
    slab = pl.program_id(0)
    x, yh, yl, z, c = (place_ref[i] for i in range(5))

    @pl.when(slab == 0)
    def _():
        copies = []
        for i, (ref, start, size) in enumerate(WEIGHT_PIECES):
            block = ((yl + i % 2) % 2 * 8 + i % 16 // 2) * 2 + (c + ref) % 2
            at = pl.multiple_of(block * 96, 96)
            copies.append(
                pltpu.make_async_copy(
                    weight_refs[ref].at[pl.ds(start, size)],
                    weight_s.at[pl.ds(at, size), pl.ds(0, 1152)],
                    sems.at[i],
                )
            )
        for i, (ref, start, size) in enumerate(TOKEN_PIECES):
            copies.append(
                pltpu.make_async_copy(
                    token_refs[ref].at[pl.ds(start, size)],
                    tokens_s.at[pl.ds(i * 64, size)],
                    sems.at[len(WEIGHT_PIECES) + i],
                )
            )
        for copy in copies:
            copy.start()
        first = x * 6
        for p in range(PAIRS):
            for j in range(2):
                head = 2 * p + j
                w1s[p, 64 * j : 64 * j + 64] = init_ref[0, head]
                w2s[p, 64 * j : 64 * j + 64] = init_ref[1, head]
                b1s[p, j : j + 1] = hidden_ref[pl.ds(first + head, 1), :]
            b2s[p] = jnp.concatenate(
                [outer_ref[pl.ds(first + 2 * p, 1), :], outer_ref[pl.ds(first + 2 * p + 1, 1), :]], axis=1
            )
        pick = lax.broadcasted_iota(jnp.int32, (24, 128), 0) == (
            first + lax.broadcasted_iota(jnp.int32, (24, 128), 1)
        )
        pick = pick & (lax.broadcasted_iota(jnp.int32, (24, 128), 1) < 6)
        weight_s[:, 1152:] = mm_tn(rate_t_ref[...], jnp.where(pick, 1.0, 0.0).astype(bf16)).astype(bf16)
        lane = lax.broadcasted_iota(jnp.int32, (1, 128), 1)
        rate_bias = jnp.zeros((1, 128), f32)
        for j in range(6):
            rate_bias = jnp.where(lane == j, rate_bias_ref[first + j], rate_bias)
        for copy in copies[: len(WEIGHT_PIECES)]:
            copy.wait()
        for i in range(4):
            for copy in copies[len(WEIGHT_PIECES) + 4 * i : len(WEIGHT_PIECES) + 4 * i + 4]:
                copy.wait()
            rows = pl.ds(i * 256, 256)
            for n in range(4):
                cols = pl.ds(n * 256, 256)
                proj_s[rows, cols] = mm(tokens_s[rows, :], weight_s[:, cols]).astype(bf16)
            rest = mm(tokens_s[rows, :], weight_s[:, 1024:])
            proj_s[rows, 1024:] = rest[:, :128].astype(bf16)
            rate_s[rows] = (1.0 / 20480.0) / (1.0 + jnp.exp(-(rest[:, 128:] + rate_bias)))

    def first_row(half):
        away = (slab // 2 - x + 4) % 4
        near = jnp.where(away == 0, 0, jnp.where(away == 3, 2, 4)) + half
        own = jnp.where(away == 2, 6 + 2 * half, near)
        below, above = (7, 13) if half else (12, 9)
        far = jnp.where(away == 3, below, jnp.where(away == 1, above, jnp.where(away == 0, 10, 14) + half))
        return jnp.where(slab % 2 == yh, own, far) * MB

    low = lax.broadcasted_iota(jnp.int32, (64, 128), 1) < 64

    def two(x):
        zero = jnp.zeros_like(x)
        return jnp.concatenate([jnp.where(low, x, zero), jnp.where(low, zero, x)], axis=0)

    tri = lax.broadcasted_iota(jnp.int32, (64, 128), 0) >= lax.broadcasted_iota(jnp.int32, (64, 128), 1) % 64

    def one(x):
        return jnp.where(low, x[:64], x[64:])

    def train(m):
        rows = pl.ds(pl.multiple_of(first_row(m), MB), MB)
        D = []
        for p in range(PAIRS):
            def part(c):
                return proj_s[rows, pl.ds(c * 384 + p * 128, 128)]
            q, k, v = part(0), part(1), part(2)
            kf = k.astype(f32)
            kmb = two(k)
            w1 = w1s[p].astype(bf16); w2 = w2s[p].astype(bf16)
            b1 = b1s[p]
            bias = jnp.concatenate([jnp.broadcast_to(b1[0:1], (64, 256)), jnp.broadcast_to(b1[1:2], (64, 256))], axis=0)
            z1 = mm(kmb, w1) + bias
            D.append(dict(w1=w1, w2=w2, kmb=kmb, q=q, vk=v.astype(f32) - kf, z1=z1, b1=b1, b2=b2s[p]))
        yield
        for p in range(PAIRS):
            d = D[p]
            z1 = d["z1"]
            s = gate(z1)
            d["x2"] = (z1 * s).astype(bf16)
            d["z2"] = mm_nt(d["x2"], d["w2"])
            d["slope"] = s + (z1 * (s - s * s)) * (2.0 * root_scale + (6.0 * root_scale * cubic) * (z1 * z1))
        yield
        for p in range(PAIRS):
            d = D[p]
            rate = jnp.where(low, rate_s[rows, 2 * p : 2 * p + 1], rate_s[rows, 2 * p + 1 : 2 * p + 2])
            h2 = (one(d["z2"]) + (d["b2"] - d["vk"])) * rate
            d["h2b"] = two(h2.astype(bf16))
            d["g1"] = mm(d["h2b"], d["w2"])
            b2n = d["b2"] - jnp.sum(h2, axis=0, keepdims=True)
            if m == 1:
                b2n = b2n.astype(bf16).astype(f32)
            b2s[p] = b2n
        for p in range(PAIRS):
            d = D[p]
            d["m1"] = two(jnp.where(tri, -1.0 - mm_nt(d["q"], d["kmb"]), 0.0).astype(bf16))
            w2n = w2s[p] - mm_tn(d["h2b"], d["x2"])
            if m == 1:
                w2n = w2n.astype(bf16).astype(f32)
            w2s[p] = w2n
        yield
        for p in range(PAIRS):
            d = D[p]
            h1 = d["g1"] * d["slope"]
            h1b = h1.astype(bf16)
            w1n = w1s[p] - mm_tn(d["kmb"], h1b)
            db = jnp.concatenate([jnp.sum(h1[:64], axis=0, keepdims=True), jnp.sum(h1[64:], axis=0, keepdims=True)], axis=0)
            b1n = d["b1"] - db
            if m == 1:
                w1n = w1n.astype(bf16).astype(f32); b1n = b1n.astype(bf16).astype(f32)
            w1s[p] = w1n; b1s[p] = b1n
            d["h1b"] = h1b
        yield
        for p in range(PAIRS):
            d = D[p]
            qm_s[m, p, :, :128] = two(d["q"])
            qm_s[m, p, :, 128:] = d["m1"]
            wh_s[m, p, :128] = d["w1"]
            wh_s[m, p, 128:] = d["h1b"]
            wx_s[m, p, :128] = d["w2"]
            wx_s[m, p, 128:] = d["x2"]
            h2_s[m, p] = d["h2b"]
            b1_s[m, p] = d["b1"]
            b2_s[m, p] = d["b2"]
            q_s[m, p] = d["q"]
        yield

    def query(m, start):
        D = [dict() for _ in range(PAIRS)]
        for p in range(PAIRS):
            b1 = b1_s[m, p]
            bias = jnp.concatenate([jnp.broadcast_to(b1[0:1], (64, 256)), jnp.broadcast_to(b1[1:2], (64, 256))], axis=0)
            D[p]["zq"] = mm(qm_s[m, p], wh_s[m, p]) + bias
        yield
        for p in range(PAIRS):
            d = D[p]
            zq = d["zq"]
            xq = (zq * gate(zq)).astype(bf16)
            both = mm_nt(xq, wx_s[m, p])
            d["bw"] = both[:, :128]
            d["bx"] = both[:, 128:]
        yield
        for p in range(PAIRS):
            d = D[p]
            m2 = jnp.where(tri, one(d["bx"]) + 1.0, 0.0).astype(bf16)
            d["mh"] = mm(m2, h2_s[m, p])
        yield
        for p in range(PAIRS):
            d = D[p]
            y = q_s[m, p].astype(f32) + (one(d["bw"]) + b2_s[m, p]) - d["mh"]
            yy = y * y
            lo = jnp.sum(jnp.where(low, yy, 0.0), axis=1, keepdims=True)
            hi = jnp.sum(jnp.where(low, 0.0, yy), axis=1, keepdims=True)
            y = y * lax.rsqrt(jnp.where(low, lo, hi) * (1.0 / 64.0) + 1e-6)
            y = y * gain_ref[0:1, p * 128 : (p + 1) * 128]
            out_ref[pl.ds(start, MB), p * 128 : (p + 1) * 128] = y.astype(bf16)
        yield

    def weave(*gens):
        gens = list(gens)
        while gens:
            for g in list(gens):
                if next(g, "end") == "end":
                    gens.remove(g)

    before = pl.multiple_of(jnp.maximum(slab * 128 - MB, 0), MB)
    weave(train(0), query(1, before))
    weave(train(1), query(0, pl.multiple_of(slab * 128, MB)))

    @pl.when(slab == 7)
    def _():
        weave(query(1, pl.multiple_of(slab * 128 + MB, MB)))


def layer(place, tokens, weights, rate_t, rate_bias, init_weights, hidden, outer, gain):
    def whole(shape):
        return pl.BlockSpec(shape, lambda i, place: (0,) * len(shape))

    far = pl.BlockSpec(memory_space=pltpu.HBM)
    anywhere = pl.BlockSpec(memory_space=pl.ANY)
    pieces = len(TOKEN_PIECES) + len(WEIGHT_PIECES)
    return pl.pallas_call(
        layer_kernel,
        out_shape=jax.ShapeDtypeStruct((1024, 384), bf16),
        grid_spec=pltpu.PrefetchScalarGridSpec(
            num_scalar_prefetch=1,
            grid=(8,),
            in_specs=[far] * (NT + 1)
            + [anywhere]
            + [
                whole((24, 3072)),
                pl.BlockSpec(memory_space=pltpu.SMEM),
                pl.BlockSpec((2, 6, 64, 256), lambda i, place: (0, place[0], 0, 0)),
                whole((24, 256)),
                whole((24, 64)),
                pl.BlockSpec((1, 384), lambda i, place: (0, place[0])),
            ],
            out_specs=whole((1024, 384)),
            scratch_shapes=[
                pltpu.VMEM((PAIRS, 128, 256), f32),
                pltpu.VMEM((PAIRS, 128, 256), f32),
                pltpu.VMEM((PAIRS, 2, 256), f32),
                pltpu.VMEM((PAIRS, 1, 128), f32),
                pltpu.VMEM((2, PAIRS, 128, 256), bf16),
                pltpu.VMEM((2, PAIRS, 256, 256), bf16),
                pltpu.VMEM((2, PAIRS, 256, 256), bf16),
                pltpu.VMEM((2, PAIRS, 128, 128), bf16),
                pltpu.VMEM((2, PAIRS, 2, 256), f32),
                pltpu.VMEM((2, PAIRS, 1, 128), f32),
                pltpu.VMEM((2, PAIRS, 64, 128), bf16),
                pltpu.VMEM((1024, 3072), bf16),
                pltpu.VMEM((3072, 1280), bf16),
                pltpu.VMEM((1024, 1152), bf16),
                pltpu.VMEM((1024, 128), f32),
                pltpu.SemaphoreType.DMA((pieces,)),
            ],
        ),
        compiler_params=pltpu.CompilerParams(
            dimension_semantics=("arbitrary",), vmem_limit_bytes=32 << 20
        ),
        name="layer",
    )(place, *tokens, *weights, rate_t, rate_bias, init_weights, hidden, outer, gain)


DP = ("yl", "z", "c")
SEQ = ("x", "yh")
swap = [(0, 1), (1, 0)]


def ring(size, step):
    return [(i, (i + step) % size) for i in range(size)]


def after(value, others):
    return lax.optimization_barrier((value, others))[0]


def on_device(
    frames,
    proj_weight,
    rate_weight,
    rate_bias,
    init_weights,
    init_bias_hidden,
    init_bias_out,
    out_gain,
):
    x, yh, yl, z, c = (lax.axis_index(name) for name in ("x", "yh", "yl", "z", "c"))

    up, down = ring(4, 1), ring(4, -1)

    part = jnp.concatenate(
        [lax.dynamic_slice(proj_weight, (0, i * 1536 + x * 384), (96, 384)) for i in range(3)], axis=1
    )
    mine = lax.dynamic_index_in_dim(frames, yh, 0, keepdims=False)
    sent = lax.dynamic_index_in_dim(frames, 1 - yh, 0, keepdims=False)
    theirs = lax.ppermute(sent, "yh", swap)
    a1, b1 = lax.ppermute(mine, "x", up), lax.ppermute(mine, "x", down)
    t0, t1, a1, b1 = lax.optimization_barrier((theirs[:64], theirs[64:], a1, b1))
    a2, b2 = lax.ppermute(t0, "x", up), lax.ppermute(t1, "x", down)
    a3 = lax.ppermute(jnp.concatenate([a1[:64], t1]), "x", up)
    b3 = lax.ppermute(jnp.concatenate([b1[64:], t0]), "x", down)
    a4, b4 = lax.ppermute(a2, "x", up), lax.ppermute(b2, "x", down)
    tokens = [mine, a1, b1, a3, b3, theirs, a2, b2, a4, b4]
    pair = jnp.concatenate([part, lax.ppermute(part, "yl", swap)])
    gathered = lax.all_gather(pair, "z", axis=0, tiled=True)
    gathered = after(gathered, (a3, b3, a4, b4))
    weights = [gathered, lax.ppermute(gathered, "c", swap)]

    result = layer(
        jnp.stack([x, yh, yl, z, c]).astype(jnp.int32), tokens, weights, rate_weight.T, rate_bias,
        init_weights, init_bias_hidden, init_bias_out, out_gain.reshape(1, 1536),
    )
    result = lax.all_to_all(result.reshape(8, 128, 384), SEQ, 0, 0, tiled=True)
    return result.reshape(4, 2, 128, 384).transpose(1, 2, 0, 3).reshape(2, 128, 1536)


def solution(mesh):
    fine = Mesh(mesh.devices.reshape(4, 2, 2, 8, 2), ("x", "yh", "yl", "z", "c"))
    return jax.shard_map(
        on_device,
        mesh=fine,
        in_specs=(P(DP, SEQ, None), P(DP, None), P(), P(), P(), P(), P(), P()),
        out_specs=P(DP, SEQ, None),
        check_vma=False,
    )
```

```python
import math

import jax
import jax.numpy as jnp
from jax import lax
from jax.experimental import pallas as pl
from jax.experimental.pallas import tpu as pltpu
from jax.sharding import Mesh
from jax.sharding import PartitionSpec as P

MB = 64
PAIRS = 3
cubic = 0.044715
root_scale = math.sqrt(2.0 / math.pi)
bf16 = jnp.bfloat16
f32 = jnp.float32


def mm(a, b):
    return lax.dot_general(a, b, (((1,), (0,)), ((), ())), preferred_element_type=f32)


def mm_nt(a, b):
    return lax.dot_general(a, b, (((1,), (1,)), ((), ())), preferred_element_type=f32)


def mm_tn(a, b):
    return lax.dot_general(a, b, (((0,), (0,)), ((), ())), preferred_element_type=f32)


def gate(z):
    return 0.5 + 0.5 * jnp.tanh(z * (root_scale + (root_scale * cubic) * (z * z)))


NT = 10
NW = 2
TOKEN_PIECES = [
    (i, j * 64, 64) for i, count in enumerate((2, 2, 2, 2, 2, 2, 1, 1, 1, 1)) for j in range(count)
]
WEIGHT_PIECES = [(h, i * 96, 96) for h in range(NW) for i in range(16)]


def layer_kernel(place_ref, *refs):
    token_refs = refs[:NT]
    weight_refs = refs[NT : NT + NW]
    rate_t_ref, rate_bias_ref, init_ref, hidden_ref, outer_ref, gain_ref, out_ref = refs[NT + NW : NT + NW + 7]
    (w1s, w2s, b1s, b2s, qm_s, wh_s, wx_s, h2_s, b1_s, b2_s, q_s,
     tokens_s, weight_s, proj_s, rate_s, sems) = refs[NT + NW + 7 :]
    slab = pl.program_id(0)
    x, yh, yl, z, c = (place_ref[i] for i in range(5))

    @pl.when(slab == 0)
    def _():
        copies = []
        for i, (ref, start, size) in enumerate(WEIGHT_PIECES):
            block = ((yl + i % 2) % 2 * 8 + i % 16 // 2) * 2 + (c + ref) % 2
            at = pl.multiple_of(block * 96, 96)
            copies.append(
                pltpu.make_async_copy(
                    weight_refs[ref].at[pl.ds(start, size)],
                    weight_s.at[pl.ds(at, size), pl.ds(0, 1152)],
                    sems.at[i],
                )
            )
        for i, (ref, start, size) in enumerate(TOKEN_PIECES):
            copies.append(
                pltpu.make_async_copy(
                    token_refs[ref].at[pl.ds(start, size)],
                    tokens_s.at[pl.ds(i * 64, size)],
                    sems.at[len(WEIGHT_PIECES) + i],
                )
            )
        for copy in copies:
            copy.start()
        first = x * 6
        for p in range(PAIRS):
            for j in range(2):
                head = 2 * p + j
                w1s[p, 64 * j : 64 * j + 64] = init_ref[0, head]
                w2s[p, 64 * j : 64 * j + 64] = init_ref[1, head]
                b1s[p, j : j + 1] = hidden_ref[pl.ds(first + head, 1), :]
            b2s[p] = jnp.concatenate(
                [outer_ref[pl.ds(first + 2 * p, 1), :], outer_ref[pl.ds(first + 2 * p + 1, 1), :]], axis=1
            )
        pick = lax.broadcasted_iota(jnp.int32, (24, 128), 0) == (
            first + lax.broadcasted_iota(jnp.int32, (24, 128), 1)
        )
        pick = pick & (lax.broadcasted_iota(jnp.int32, (24, 128), 1) < 6)
        weight_s[:, 1152:] = mm_tn(rate_t_ref[...], jnp.where(pick, 1.0, 0.0).astype(bf16)).astype(bf16)
        lane = lax.broadcasted_iota(jnp.int32, (1, 128), 1)
        rate_bias = jnp.zeros((1, 128), f32)
        for j in range(6):
            rate_bias = jnp.where(lane == j, rate_bias_ref[first + j], rate_bias)
        for copy in copies[: len(WEIGHT_PIECES)]:
            copy.wait()
        for i in range(4):
            for copy in copies[len(WEIGHT_PIECES) + 4 * i : len(WEIGHT_PIECES) + 4 * i + 4]:
                copy.wait()
            rows = pl.ds(i * 256, 256)
            for n in range(4):
                cols = pl.ds(n * 256, 256)
                proj_s[rows, cols] = mm(tokens_s[rows, :], weight_s[:, cols]).astype(bf16)
            rest = mm(tokens_s[rows, :], weight_s[:, 1024:])
            proj_s[rows, 1024:] = rest[:, :128].astype(bf16)
            rate_s[rows] = (1.0 / 20480.0) / (1.0 + jnp.exp(-(rest[:, 128:] + rate_bias)))

    def first_row(half):
        away = (slab // 2 - x + 4) % 4
        near = jnp.where(away == 0, 0, jnp.where(away == 3, 2, 4)) + half
        own = jnp.where(away == 2, 6 + 2 * half, near)
        below, above = (7, 13) if half else (12, 9)
        far = jnp.where(away == 3, below, jnp.where(away == 1, above, jnp.where(away == 0, 10, 14) + half))
        return jnp.where(slab % 2 == yh, own, far) * MB

    low = lax.broadcasted_iota(jnp.int32, (64, 128), 1) < 64

    def two(x):
        zero = jnp.zeros_like(x)
        return jnp.concatenate([jnp.where(low, x, zero), jnp.where(low, zero, x)], axis=0)

    tri = lax.broadcasted_iota(jnp.int32, (64, 128), 0) >= lax.broadcasted_iota(jnp.int32, (64, 128), 1) % 64

    def one(x):
        return jnp.where(low, x[:64], x[64:])

    def train(m):
        rows = pl.ds(pl.multiple_of(first_row(m), MB), MB)
        D = []
        for p in range(PAIRS):
            def part(c):
                return proj_s[rows, pl.ds(c * 384 + p * 128, 128)]
            q, k, v = part(0), part(1), part(2)
            kf = k.astype(f32)
            kmb = two(k)
            w1 = w1s[p].astype(bf16); w2 = w2s[p].astype(bf16)
            b1 = b1s[p]
            bias = jnp.concatenate([jnp.broadcast_to(b1[0:1], (64, 256)), jnp.broadcast_to(b1[1:2], (64, 256))], axis=0)
            z1 = mm(kmb, w1) + bias
            D.append(dict(w1=w1, w2=w2, kmb=kmb, q=q, vk=v.astype(f32) - kf, z1=z1, b1=b1, b2=b2s[p]))
        yield
        for p in range(PAIRS):
            d = D[p]
            z1 = d["z1"]
            s = gate(z1)
            d["x2"] = (z1 * s).astype(bf16)
            d["z2"] = mm_nt(d["x2"], d["w2"])
            d["slope"] = s + (z1 * (s - s * s)) * (2.0 * root_scale + (6.0 * root_scale * cubic) * (z1 * z1))
        yield
        for p in range(PAIRS):
            d = D[p]
            rate = jnp.where(low, rate_s[rows, 2 * p : 2 * p + 1], rate_s[rows, 2 * p + 1 : 2 * p + 2])
            h2 = (one(d["z2"]) + (d["b2"] - d["vk"])) * rate
            d["h2b"] = two(h2.astype(bf16))
            d["g1"] = mm(d["h2b"], d["w2"])
            b2n = d["b2"] - jnp.sum(h2, axis=0, keepdims=True)
            if m == 1:
                b2n = b2n.astype(bf16).astype(f32)
            b2s[p] = b2n
        for p in range(PAIRS):
            d = D[p]
            d["m1"] = two(jnp.where(tri, -1.0 - mm_nt(d["q"], d["kmb"]), 0.0).astype(bf16))
            w2n = w2s[p] - mm_tn(d["h2b"], d["x2"])
            if m == 1:
                w2n = w2n.astype(bf16).astype(f32)
            w2s[p] = w2n
        yield
        for p in range(PAIRS):
            d = D[p]
            h1 = d["g1"] * d["slope"]
            h1b = h1.astype(bf16)
            w1n = w1s[p] - mm_tn(d["kmb"], h1b)
            db = jnp.concatenate([jnp.sum(h1[:64], axis=0, keepdims=True), jnp.sum(h1[64:], axis=0, keepdims=True)], axis=0)
            b1n = d["b1"] - db
            if m == 1:
                w1n = w1n.astype(bf16).astype(f32); b1n = b1n.astype(bf16).astype(f32)
            w1s[p] = w1n; b1s[p] = b1n
            d["h1b"] = h1b
        yield
        for p in range(PAIRS):
            d = D[p]
            qm_s[m, p, :, :128] = two(d["q"])
            qm_s[m, p, :, 128:] = d["m1"]
            wh_s[m, p, :128] = d["w1"]
            wh_s[m, p, 128:] = d["h1b"]
            wx_s[m, p, :128] = d["w2"]
            wx_s[m, p, 128:] = d["x2"]
            h2_s[m, p] = d["h2b"]
            b1_s[m, p] = d["b1"]
            b2_s[m, p] = d["b2"]
            q_s[m, p] = d["q"]
        yield

    def query(m, start):
        D = [dict() for _ in range(PAIRS)]
        for p in range(PAIRS):
            b1 = b1_s[m, p]
            bias = jnp.concatenate([jnp.broadcast_to(b1[0:1], (64, 256)), jnp.broadcast_to(b1[1:2], (64, 256))], axis=0)
            D[p]["zq"] = mm(qm_s[m, p], wh_s[m, p]) + bias
        yield
        for p in range(PAIRS):
            d = D[p]
            zq = d["zq"]
            xq = (zq * gate(zq)).astype(bf16)
            both = mm_nt(xq, wx_s[m, p])
            d["bw"] = both[:, :128]
            d["bx"] = both[:, 128:]
        yield
        for p in range(PAIRS):
            d = D[p]
            m2 = jnp.where(tri, one(d["bx"]) + 1.0, 0.0).astype(bf16)
            d["mh"] = mm(m2, h2_s[m, p])
        yield
        for p in range(PAIRS):
            d = D[p]
            y = q_s[m, p].astype(f32) + (one(d["bw"]) + b2_s[m, p]) - d["mh"]
            yy = y * y
            lo = jnp.sum(jnp.where(low, yy, 0.0), axis=1, keepdims=True)
            hi = jnp.sum(jnp.where(low, 0.0, yy), axis=1, keepdims=True)
            y = y * lax.rsqrt(jnp.where(low, lo, hi) * (1.0 / 64.0) + 1e-6)
            y = y * gain_ref[0:1, p * 128 : (p + 1) * 128]
            out_ref[pl.ds(start, MB), p * 128 : (p + 1) * 128] = y.astype(bf16)
        yield

    def weave(*gens):
        gens = list(gens)
        while gens:
            for g in list(gens):
                if next(g, "end") == "end":
                    gens.remove(g)

    before = pl.multiple_of(jnp.maximum(slab * 128 - MB, 0), MB)
    weave(train(0), query(1, before))
    weave(train(1), query(0, pl.multiple_of(slab * 128, MB)))

    @pl.when(slab == 7)
    def _():
        weave(query(1, pl.multiple_of(slab * 128 + MB, MB)))


def layer(place, tokens, weights, rate_t, rate_bias, init_weights, hidden, outer, gain):
    def whole(shape):
        return pl.BlockSpec(shape, lambda i, place: (0,) * len(shape))

    far = pl.BlockSpec(memory_space=pltpu.HBM)
    anywhere = pl.BlockSpec(memory_space=pl.ANY)
    pieces = len(TOKEN_PIECES) + len(WEIGHT_PIECES)
    return pl.pallas_call(
        layer_kernel,
        out_shape=jax.ShapeDtypeStruct((1024, 384), bf16),
        grid_spec=pltpu.PrefetchScalarGridSpec(
            num_scalar_prefetch=1,
            grid=(8,),
            in_specs=[far] * (NT + 1)
            + [anywhere]
            + [
                whole((24, 3072)),
                pl.BlockSpec(memory_space=pltpu.SMEM),
                pl.BlockSpec((2, 6, 64, 256), lambda i, place: (0, place[0], 0, 0)),
                whole((24, 256)),
                whole((24, 64)),
                pl.BlockSpec((1, 384), lambda i, place: (0, place[0])),
            ],
            out_specs=whole((1024, 384)),
            scratch_shapes=[
                pltpu.VMEM((PAIRS, 128, 256), f32),
                pltpu.VMEM((PAIRS, 128, 256), f32),
                pltpu.VMEM((PAIRS, 2, 256), f32),
                pltpu.VMEM((PAIRS, 1, 128), f32),
                pltpu.VMEM((2, PAIRS, 128, 256), bf16),
                pltpu.VMEM((2, PAIRS, 256, 256), bf16),
                pltpu.VMEM((2, PAIRS, 256, 256), bf16),
                pltpu.VMEM((2, PAIRS, 128, 128), bf16),
                pltpu.VMEM((2, PAIRS, 2, 256), f32),
                pltpu.VMEM((2, PAIRS, 1, 128), f32),
                pltpu.VMEM((2, PAIRS, 64, 128), bf16),
                pltpu.VMEM((1024, 3072), bf16),
                pltpu.VMEM((3072, 1280), bf16),
                pltpu.VMEM((1024, 1152), bf16),
                pltpu.VMEM((1024, 128), f32),
                pltpu.SemaphoreType.DMA((pieces,)),
            ],
        ),
        compiler_params=pltpu.CompilerParams(
            dimension_semantics=("arbitrary",), vmem_limit_bytes=60 << 20
        ),
        name="layer",
    )(place, *tokens, *weights, rate_t, rate_bias, init_weights, hidden, outer, gain)


DP = ("yl", "z", "c")
SEQ = ("x", "yh")
swap = [(0, 1), (1, 0)]


def ring(size, step):
    return [(i, (i + step) % size) for i in range(size)]


def after(value, others):
    return lax.optimization_barrier((value, others))[0]


def on_device(
    frames,
    proj_weight,
    rate_weight,
    rate_bias,
    init_weights,
    init_bias_hidden,
    init_bias_out,
    out_gain,
):
    x, yh, yl, z, c = (lax.axis_index(name) for name in ("x", "yh", "yl", "z", "c"))

    up, down = ring(4, 1), ring(4, -1)

    part = jnp.concatenate(
        [lax.dynamic_slice(proj_weight, (0, i * 1536 + x * 384), (96, 384)) for i in range(3)], axis=1
    )
    mine = lax.dynamic_index_in_dim(frames, yh, 0, keepdims=False)
    sent = lax.dynamic_index_in_dim(frames, 1 - yh, 0, keepdims=False)
    theirs = lax.ppermute(sent, "yh", swap)
    a1, b1 = lax.ppermute(mine, "x", up), lax.ppermute(mine, "x", down)
    t0, t1, a1, b1 = lax.optimization_barrier((theirs[:64], theirs[64:], a1, b1))
    a2, b2 = lax.ppermute(t0, "x", up), lax.ppermute(t1, "x", down)
    a3 = lax.ppermute(jnp.concatenate([a1[:64], t1]), "x", up)
    b3 = lax.ppermute(jnp.concatenate([b1[64:], t0]), "x", down)
    a4, b4 = lax.ppermute(a2, "x", up), lax.ppermute(b2, "x", down)
    tokens = [mine, a1, b1, a3, b3, theirs, a2, b2, a4, b4]
    pair = jnp.concatenate([part, lax.ppermute(part, "yl", swap)])
    gathered = lax.all_gather(pair, "z", axis=0, tiled=True)
    gathered = after(gathered, (a2, b2, a3, b3))
    weights = [gathered, lax.ppermute(gathered, "c", swap)]

    result = layer(
        jnp.stack([x, yh, yl, z, c]).astype(jnp.int32), tokens, weights, rate_weight.T, rate_bias,
        init_weights, init_bias_hidden, init_bias_out, out_gain.reshape(1, 1536),
    )
    result = lax.all_to_all(result.reshape(8, 128, 384), SEQ, 0, 0, tiled=True)
    result = result.reshape(4, 2, 128, 384)
    return jnp.concatenate([result[i] for i in range(4)], axis=2)


def solution(mesh):
    fine = Mesh(mesh.devices.reshape(4, 2, 2, 8, 2), ("x", "yh", "yl", "z", "c"))
    return jax.shard_map(
        on_device,
        mesh=fine,
        in_specs=(P(DP, SEQ, None), P(DP, None), P(), P(), P(), P(), P(), P()),
        out_specs=P(DP, SEQ, None),
        check_vma=False,
    )
```

```python
import math

import jax
import jax.numpy as jnp
from jax import lax
from jax.experimental import pallas as pl
from jax.experimental.pallas import tpu as pltpu
from jax.sharding import Mesh
from jax.sharding import PartitionSpec as P

MB = 64
PAIRS = 3
cubic = 0.044715
root_scale = math.sqrt(2.0 / math.pi)
bf16 = jnp.bfloat16
f32 = jnp.float32


def mm(a, b):
    return lax.dot_general(a, b, (((1,), (0,)), ((), ())), preferred_element_type=f32)


def mm_nt(a, b):
    return lax.dot_general(a, b, (((1,), (1,)), ((), ())), preferred_element_type=f32)


def mm_tn(a, b):
    return lax.dot_general(a, b, (((0,), (0,)), ((), ())), preferred_element_type=f32)


def gate(z):
    return 0.5 + 0.5 * jnp.tanh(z * (root_scale + (root_scale * cubic) * (z * z)))


NT = 10
NW = 2
TOKEN_PIECES = [
    (i, j * 64, 64) for i, count in enumerate((2, 2, 2, 2, 2, 2, 1, 1, 1, 1)) for j in range(count)
]
WEIGHT_PIECES = [(h, i * 96, 96) for h in range(NW) for i in range(16)]


def layer_kernel(place_ref, *refs):
    token_refs = refs[:NT]
    weight_refs = refs[NT : NT + NW]
    rate_t_ref, rate_bias_ref, init_ref, hidden_ref, outer_ref, gain_ref, out_ref = refs[NT + NW : NT + NW + 7]
    (w1s, w2s, b1s, b2s, qm_s, wh_s, wx_s, h2_s, b1_s, b2_s, q_s,
     tokens_s, weight_s, proj_s, rate_s, sems) = refs[NT + NW + 7 :]
    slab = pl.program_id(0)
    x, yh, yl, z, c = (place_ref[i] for i in range(5))

    @pl.when(slab == 0)
    def _():
        copies = []
        for i, (ref, start, size) in enumerate(WEIGHT_PIECES):
            block = ((yl + i % 2) % 2 * 8 + i % 16 // 2) * 2 + (c + ref) % 2
            at = pl.multiple_of(block * 96, 96)
            copies.append(
                pltpu.make_async_copy(
                    weight_refs[ref].at[pl.ds(start, size)],
                    weight_s.at[pl.ds(at, size), pl.ds(0, 1152)],
                    sems.at[i],
                )
            )
        for i, (ref, start, size) in enumerate(TOKEN_PIECES):
            copies.append(
                pltpu.make_async_copy(
                    token_refs[ref].at[pl.ds(start, size)],
                    tokens_s.at[pl.ds(i * 64, size)],
                    sems.at[len(WEIGHT_PIECES) + i],
                )
            )
        early = len(WEIGHT_PIECES) + 4
        for copy in copies[:early]:
            copy.start()
        first = x * 6
        for p in range(PAIRS):
            for j in range(2):
                head = 2 * p + j
                w1s[p, 64 * j : 64 * j + 64] = init_ref[0, head]
                w2s[p, 64 * j : 64 * j + 64] = init_ref[1, head]
                b1s[p, j : j + 1] = hidden_ref[pl.ds(first + head, 1), :]
            b2s[p] = jnp.concatenate(
                [outer_ref[pl.ds(first + 2 * p, 1), :], outer_ref[pl.ds(first + 2 * p + 1, 1), :]], axis=1
            )
        pick = lax.broadcasted_iota(jnp.int32, (24, 128), 0) == (
            first + lax.broadcasted_iota(jnp.int32, (24, 128), 1)
        )
        pick = pick & (lax.broadcasted_iota(jnp.int32, (24, 128), 1) < 6)
        weight_s[:, 1152:] = mm_tn(rate_t_ref[...], jnp.where(pick, 1.0, 0.0).astype(bf16)).astype(bf16)
        lane = lax.broadcasted_iota(jnp.int32, (1, 128), 1)
        rate_bias = jnp.zeros((1, 128), f32)
        for j in range(6):
            rate_bias = jnp.where(lane == j, rate_bias_ref[first + j], rate_bias)
        for copy in copies[: len(WEIGHT_PIECES)]:
            copy.wait()
        for copy in copies[early:]:
            copy.start()
        for i in range(4):
            for copy in copies[len(WEIGHT_PIECES) + 4 * i : len(WEIGHT_PIECES) + 4 * i + 4]:
                copy.wait()
            rows = pl.ds(i * 256, 256)
            for n in range(4):
                cols = pl.ds(n * 256, 256)
                proj_s[rows, cols] = mm(tokens_s[rows, :], weight_s[:, cols]).astype(bf16)
            rest = mm(tokens_s[rows, :], weight_s[:, 1024:])
            proj_s[rows, 1024:] = rest[:, :128].astype(bf16)
            rate_s[rows] = (1.0 / 20480.0) / (1.0 + jnp.exp(-(rest[:, 128:] + rate_bias)))

    def first_row(half):
        away = (slab // 2 - x + 4) % 4
        near = jnp.where(away == 0, 0, jnp.where(away == 3, 2, 4)) + half
        own = jnp.where(away == 2, 6 + 2 * half, near)
        below, above = (7, 13) if half else (12, 9)
        far = jnp.where(away == 3, below, jnp.where(away == 1, above, jnp.where(away == 0, 10, 14) + half))
        return jnp.where(slab % 2 == yh, own, far) * MB

    low = lax.broadcasted_iota(jnp.int32, (64, 128), 1) < 64

    def two(x):
        zero = jnp.zeros_like(x)
        return jnp.concatenate([jnp.where(low, x, zero), jnp.where(low, zero, x)], axis=0)

    tri = lax.broadcasted_iota(jnp.int32, (64, 128), 0) >= lax.broadcasted_iota(jnp.int32, (64, 128), 1) % 64

    def one(x):
        return jnp.where(low, x[:64], x[64:])

    def train(m):
        rows = pl.ds(pl.multiple_of(first_row(m), MB), MB)
        D = []
        for p in range(PAIRS):
            def part(c):
                return proj_s[rows, pl.ds(c * 384 + p * 128, 128)]
            q, k, v = part(0), part(1), part(2)
            kf = k.astype(f32)
            kmb = two(k)
            w1 = w1s[p].astype(bf16); w2 = w2s[p].astype(bf16)
            b1 = b1s[p]
            bias = jnp.concatenate([jnp.broadcast_to(b1[0:1], (64, 256)), jnp.broadcast_to(b1[1:2], (64, 256))], axis=0)
            z1 = mm(kmb, w1) + bias
            D.append(dict(w1=w1, w2=w2, kmb=kmb, q=q, vk=v.astype(f32) - kf, z1=z1, b1=b1, b2=b2s[p]))
        yield
        for p in range(PAIRS):
            d = D[p]
            z1 = d["z1"]
            s = gate(z1)
            d["x2"] = (z1 * s).astype(bf16)
            d["z2"] = mm_nt(d["x2"], d["w2"])
            d["slope"] = s + (z1 * (s - s * s)) * (2.0 * root_scale + (6.0 * root_scale * cubic) * (z1 * z1))
        yield
        for p in range(PAIRS):
            d = D[p]
            rate = jnp.where(low, rate_s[rows, 2 * p : 2 * p + 1], rate_s[rows, 2 * p + 1 : 2 * p + 2])
            h2 = (one(d["z2"]) + (d["b2"] - d["vk"])) * rate
            d["h2b"] = two(h2.astype(bf16))
            d["g1"] = mm(d["h2b"], d["w2"])
            b2n = d["b2"] - jnp.sum(h2, axis=0, keepdims=True)
            if m == 1:
                b2n = b2n.astype(bf16).astype(f32)
            b2s[p] = b2n
        for p in range(PAIRS):
            d = D[p]
            d["m1"] = two(jnp.where(tri, -1.0 - mm_nt(d["q"], d["kmb"]), 0.0).astype(bf16))
            w2n = w2s[p] - mm_tn(d["h2b"], d["x2"])
            if m == 1:
                w2n = w2n.astype(bf16).astype(f32)
            w2s[p] = w2n
        yield
        for p in range(PAIRS):
            d = D[p]
            h1 = d["g1"] * d["slope"]
            h1b = h1.astype(bf16)
            w1n = w1s[p] - mm_tn(d["kmb"], h1b)
            db = jnp.concatenate([jnp.sum(h1[:64], axis=0, keepdims=True), jnp.sum(h1[64:], axis=0, keepdims=True)], axis=0)
            b1n = d["b1"] - db
            if m == 1:
                w1n = w1n.astype(bf16).astype(f32); b1n = b1n.astype(bf16).astype(f32)
            w1s[p] = w1n; b1s[p] = b1n
            d["h1b"] = h1b
        yield
        for p in range(PAIRS):
            d = D[p]
            qm_s[m, p, :, :128] = two(d["q"])
            qm_s[m, p, :, 128:] = d["m1"]
            wh_s[m, p, :128] = d["w1"]
            wh_s[m, p, 128:] = d["h1b"]
            wx_s[m, p, :128] = d["w2"]
            wx_s[m, p, 128:] = d["x2"]
            h2_s[m, p] = d["h2b"]
            b1_s[m, p] = d["b1"]
            b2_s[m, p] = d["b2"]
            q_s[m, p] = d["q"]
        yield

    def query(m, start):
        D = [dict() for _ in range(PAIRS)]
        for p in range(PAIRS):
            b1 = b1_s[m, p]
            bias = jnp.concatenate([jnp.broadcast_to(b1[0:1], (64, 256)), jnp.broadcast_to(b1[1:2], (64, 256))], axis=0)
            D[p]["zq"] = mm(qm_s[m, p], wh_s[m, p]) + bias
        yield
        for p in range(PAIRS):
            d = D[p]
            zq = d["zq"]
            xq = (zq * gate(zq)).astype(bf16)
            both = mm_nt(xq, wx_s[m, p])
            d["bw"] = both[:, :128]
            d["bx"] = both[:, 128:]
        yield
        for p in range(PAIRS):
            d = D[p]
            m2 = jnp.where(tri, one(d["bx"]) + 1.0, 0.0).astype(bf16)
            d["mh"] = mm(m2, h2_s[m, p])
        yield
        for p in range(PAIRS):
            d = D[p]
            y = q_s[m, p].astype(f32) + (one(d["bw"]) + b2_s[m, p]) - d["mh"]
            yy = y * y
            lo = jnp.sum(jnp.where(low, yy, 0.0), axis=1, keepdims=True)
            hi = jnp.sum(jnp.where(low, 0.0, yy), axis=1, keepdims=True)
            y = y * lax.rsqrt(jnp.where(low, lo, hi) * (1.0 / 64.0) + 1e-6)
            y = y * gain_ref[0:1, p * 128 : (p + 1) * 128]
            out_ref[pl.ds(start, MB), p * 128 : (p + 1) * 128] = y.astype(bf16)
        yield

    def weave(*gens):
        gens = list(gens)
        while gens:
            for g in list(gens):
                if next(g, "end") == "end":
                    gens.remove(g)

    before = pl.multiple_of(jnp.maximum(slab * 128 - MB, 0), MB)
    weave(train(0), query(1, before))
    weave(train(1), query(0, pl.multiple_of(slab * 128, MB)))

    @pl.when(slab == 7)
    def _():
        weave(query(1, pl.multiple_of(slab * 128 + MB, MB)))


def layer(place, tokens, weights, rate_t, rate_bias, init_weights, hidden, outer, gain):
    def whole(shape):
        return pl.BlockSpec(shape, lambda i, place: (0,) * len(shape))

    far = pl.BlockSpec(memory_space=pltpu.HBM)
    anywhere = pl.BlockSpec(memory_space=pl.ANY)
    pieces = len(TOKEN_PIECES) + len(WEIGHT_PIECES)
    return pl.pallas_call(
        layer_kernel,
        out_shape=jax.ShapeDtypeStruct((1024, 384), bf16),
        grid_spec=pltpu.PrefetchScalarGridSpec(
            num_scalar_prefetch=1,
            grid=(8,),
            in_specs=[far] * (NT + 1)
            + [anywhere]
            + [
                whole((24, 3072)),
                pl.BlockSpec(memory_space=pltpu.SMEM),
                pl.BlockSpec((2, 6, 64, 256), lambda i, place: (0, place[0], 0, 0)),
                whole((24, 256)),
                whole((24, 64)),
                pl.BlockSpec((1, 384), lambda i, place: (0, place[0])),
            ],
            out_specs=whole((1024, 384)),
            scratch_shapes=[
                pltpu.VMEM((PAIRS, 128, 256), f32),
                pltpu.VMEM((PAIRS, 128, 256), f32),
                pltpu.VMEM((PAIRS, 2, 256), f32),
                pltpu.VMEM((PAIRS, 1, 128), f32),
                pltpu.VMEM((2, PAIRS, 128, 256), bf16),
                pltpu.VMEM((2, PAIRS, 256, 256), bf16),
                pltpu.VMEM((2, PAIRS, 256, 256), bf16),
                pltpu.VMEM((2, PAIRS, 128, 128), bf16),
                pltpu.VMEM((2, PAIRS, 2, 256), f32),
                pltpu.VMEM((2, PAIRS, 1, 128), f32),
                pltpu.VMEM((2, PAIRS, 64, 128), bf16),
                pltpu.VMEM((1024, 3072), bf16),
                pltpu.VMEM((3072, 1280), bf16),
                pltpu.VMEM((1024, 1152), bf16),
                pltpu.VMEM((1024, 128), f32),
                pltpu.SemaphoreType.DMA((pieces,)),
            ],
        ),
        compiler_params=pltpu.CompilerParams(
            dimension_semantics=("arbitrary",), vmem_limit_bytes=60 << 20
        ),
        name="layer",
    )(place, *tokens, *weights, rate_t, rate_bias, init_weights, hidden, outer, gain)


DP = ("yl", "z", "c")
SEQ = ("x", "yh")
swap = [(0, 1), (1, 0)]


def ring(size, step):
    return [(i, (i + step) % size) for i in range(size)]


def after(value, others):
    return lax.optimization_barrier((value, others))[0]


def on_device(
    frames,
    proj_weight,
    rate_weight,
    rate_bias,
    init_weights,
    init_bias_hidden,
    init_bias_out,
    out_gain,
):
    x, yh, yl, z, c = (lax.axis_index(name) for name in ("x", "yh", "yl", "z", "c"))

    up, down = ring(4, 1), ring(4, -1)

    part = jnp.concatenate(
        [lax.dynamic_slice(proj_weight, (0, i * 1536 + x * 384), (96, 384)) for i in range(3)], axis=1
    )
    mine = lax.dynamic_index_in_dim(frames, yh, 0, keepdims=False)
    sent = lax.dynamic_index_in_dim(frames, 1 - yh, 0, keepdims=False)
    theirs = lax.ppermute(sent, "yh", swap)
    a1, b1 = lax.ppermute(mine, "x", up), lax.ppermute(mine, "x", down)
    t0, t1, a1, b1 = lax.optimization_barrier((theirs[:64], theirs[64:], a1, b1))
    a2, b2 = lax.ppermute(t0, "x", up), lax.ppermute(t1, "x", down)
    a3 = lax.ppermute(jnp.concatenate([a1[:64], t1]), "x", up)
    b3 = lax.ppermute(jnp.concatenate([b1[64:], t0]), "x", down)
    a4, b4 = lax.ppermute(a2, "x", up), lax.ppermute(b2, "x", down)
    tokens = [mine, a1, b1, a3, b3, theirs, a2, b2, a4, b4]
    pair = jnp.concatenate([part, lax.ppermute(part, "yl", swap)])
    gathered = lax.all_gather(pair, "z", axis=0, tiled=True)
    gathered = after(gathered, (a2, b2, a3, b3))
    weights = [gathered, lax.ppermute(gathered, "c", swap)]

    result = layer(
        jnp.stack([x, yh, yl, z, c]).astype(jnp.int32), tokens, weights, rate_weight.T, rate_bias,
        init_weights, init_bias_hidden, init_bias_out, out_gain.reshape(1, 1536),
    )
    result = lax.all_to_all(result.reshape(8, 128, 384), SEQ, 0, 0, tiled=True)
    result = result.reshape(4, 2, 128, 384)
    return jnp.concatenate([result[i] for i in range(4)], axis=2)


def solution(mesh):
    fine = Mesh(mesh.devices.reshape(4, 2, 2, 8, 2), ("x", "yh", "yl", "z", "c"))
    return jax.shard_map(
        on_device,
        mesh=fine,
        in_specs=(P(DP, SEQ, None), P(DP, None), P(), P(), P(), P(), P(), P()),
        out_specs=P(DP, SEQ, None),
        check_vma=False,
    )
```

```python
import math

import jax
import jax.numpy as jnp
from jax import lax
from jax.experimental import pallas as pl
from jax.experimental.pallas import tpu as pltpu
from jax.sharding import Mesh
from jax.sharding import PartitionSpec as P

MB = 64
PAIRS = 3
cubic = 0.044715
root_scale = math.sqrt(2.0 / math.pi)
bf16 = jnp.bfloat16
f32 = jnp.float32


def mm(a, b):
    return lax.dot_general(a, b, (((1,), (0,)), ((), ())), preferred_element_type=f32)


def mm_nt(a, b):
    return lax.dot_general(a, b, (((1,), (1,)), ((), ())), preferred_element_type=f32)


def mm_tn(a, b):
    return lax.dot_general(a, b, (((0,), (0,)), ((), ())), preferred_element_type=f32)


def gate(z):
    return 0.5 + 0.5 * jnp.tanh(z * (root_scale + (root_scale * cubic) * (z * z)))


NT = 10
NW = 2
TOKEN_PIECES = [
    (i, j * 64, 64) for i, count in enumerate((2, 2, 2, 2, 2, 2, 1, 1, 1, 1)) for j in range(count)
]
WEIGHT_PIECES = [(h, i * 96, 96) for h in range(NW) for i in range(16)]


def layer_kernel(place_ref, *refs):
    token_refs = refs[:NT]
    weight_refs = refs[NT : NT + NW]
    rate_t_ref, rate_bias_ref, init_ref, hidden_ref, outer_ref, gain_ref, out_ref = refs[NT + NW : NT + NW + 7]
    (w1s, w2s, b1s, b2s, qm_s, wh_s, wx_s, h2_s, b1_s, b2_s, q_s,
     tokens_s, weight_s, proj_s, rate_s, sems) = refs[NT + NW + 7 :]
    slab = pl.program_id(0)
    x, yh, yl, z, c = (place_ref[i] for i in range(5))

    @pl.when(slab == 0)
    def _():
        copies = []
        for i, (ref, start, size) in enumerate(WEIGHT_PIECES):
            block = ((yl + i % 2) % 2 * 8 + i % 16 // 2) * 2 + (c + ref) % 2
            at = pl.multiple_of(block * 96, 96)
            copies.append(
                pltpu.make_async_copy(
                    weight_refs[ref].at[pl.ds(start, size)],
                    weight_s.at[pl.ds(at, size), pl.ds(0, 1152)],
                    sems.at[i],
                )
            )
        for i, (ref, start, size) in enumerate(TOKEN_PIECES):
            copies.append(
                pltpu.make_async_copy(
                    token_refs[ref].at[pl.ds(start, size)],
                    tokens_s.at[pl.ds(i * 64, size)],
                    sems.at[len(WEIGHT_PIECES) + i],
                )
            )
        for copy in copies:
            copy.start()
        first = x * 6
        for p in range(PAIRS):
            for j in range(2):
                head = 2 * p + j
                w1s[p, 64 * j : 64 * j + 64] = init_ref[0, head]
                w2s[p, 64 * j : 64 * j + 64] = init_ref[1, head]
                b1s[p, j : j + 1] = hidden_ref[pl.ds(first + head, 1), :]
            b2s[p] = jnp.concatenate(
                [outer_ref[pl.ds(first + 2 * p, 1), :], outer_ref[pl.ds(first + 2 * p + 1, 1), :]], axis=1
            )
        pick = lax.broadcasted_iota(jnp.int32, (24, 128), 0) == (
            first + lax.broadcasted_iota(jnp.int32, (24, 128), 1)
        )
        pick = pick & (lax.broadcasted_iota(jnp.int32, (24, 128), 1) < 6)
        weight_s[:, 1152:] = mm_tn(rate_t_ref[...], jnp.where(pick, 1.0, 0.0).astype(bf16)).astype(bf16)
        lane = lax.broadcasted_iota(jnp.int32, (1, 128), 1)
        rate_bias = jnp.zeros((1, 128), f32)
        for j in range(6):
            rate_bias = jnp.where(lane == j, rate_bias_ref[first + j], rate_bias)
        for copy in copies[: len(WEIGHT_PIECES)]:
            copy.wait()
        for i in range(4):
            for copy in copies[len(WEIGHT_PIECES) + 4 * i : len(WEIGHT_PIECES) + 4 * i + 4]:
                copy.wait()
            rows = pl.ds(i * 256, 256)
            for n in range(4):
                cols = pl.ds(n * 256, 256)
                proj_s[rows, cols] = mm(tokens_s[rows, :], weight_s[:, cols]).astype(bf16)
            rest = mm(tokens_s[rows, :], weight_s[:, 1024:])
            proj_s[rows, 1024:] = rest[:, :128].astype(bf16)
            rate_s[rows] = (1.0 / 20480.0) / (1.0 + jnp.exp(-(rest[:, 128:] + rate_bias)))

    def first_row(half):
        away = (slab // 2 - x + 4) % 4
        near = jnp.where(away == 0, 0, jnp.where(away == 3, 2, 4)) + half
        own = jnp.where(away == 2, 6 + 2 * half, near)
        below, above = (7, 13) if half else (12, 9)
        far = jnp.where(away == 3, below, jnp.where(away == 1, above, jnp.where(away == 0, 10, 14) + half))
        return jnp.where(slab % 2 == yh, own, far) * MB

    low = lax.broadcasted_iota(jnp.int32, (64, 128), 1) < 64

    def two(x):
        zero = jnp.zeros_like(x)
        return jnp.concatenate([jnp.where(low, x, zero), jnp.where(low, zero, x)], axis=0)

    tri = lax.broadcasted_iota(jnp.int32, (64, 128), 0) >= lax.broadcasted_iota(jnp.int32, (64, 128), 1) % 64

    def one(x):
        return jnp.where(low, x[:64], x[64:])

    def train(m):
        rows = pl.ds(pl.multiple_of(first_row(m), MB), MB)
        D = []
        for p in range(PAIRS):
            def part(c):
                return proj_s[rows, pl.ds(c * 384 + p * 128, 128)]
            q, k, v = part(0), part(1), part(2)
            kf = k.astype(f32)
            kmb = two(k)
            w1 = w1s[p].astype(bf16); w2 = w2s[p].astype(bf16)
            b1 = b1s[p]
            bias = jnp.concatenate([jnp.broadcast_to(b1[0:1], (64, 256)), jnp.broadcast_to(b1[1:2], (64, 256))], axis=0)
            z1 = mm(kmb, w1) + bias
            D.append(dict(w1=w1, w2=w2, kmb=kmb, q=q, vk=v.astype(f32) - kf, z1=z1, b1=b1, b2=b2s[p]))
        yield
        for p in range(PAIRS):
            d = D[p]
            z1 = d["z1"]
            s = gate(z1)
            d["x2"] = (z1 * s).astype(bf16)
            d["z2"] = mm_nt(d["x2"], d["w2"])
            d["slope"] = s + (z1 * (s - s * s)) * (2.0 * root_scale + (6.0 * root_scale * cubic) * (z1 * z1))
        yield
        for p in range(PAIRS):
            d = D[p]
            rate = jnp.where(low, rate_s[rows, 2 * p : 2 * p + 1], rate_s[rows, 2 * p + 1 : 2 * p + 2])
            h2 = (one(d["z2"]) + (d["b2"] - d["vk"])) * rate
            d["h2b"] = two(h2.astype(bf16))
            d["g1"] = mm(d["h2b"], d["w2"])
            b2n = d["b2"] - jnp.sum(h2, axis=0, keepdims=True)
            if m == 1:
                b2n = b2n.astype(bf16).astype(f32)
            b2s[p] = b2n
        for p in range(PAIRS):
            d = D[p]
            d["m1"] = two(jnp.where(tri, -1.0 - mm_nt(d["q"], d["kmb"]), 0.0).astype(bf16))
            w2n = w2s[p] - mm_tn(d["h2b"], d["x2"])
            if m == 1:
                w2n = w2n.astype(bf16).astype(f32)
            w2s[p] = w2n
        yield
        for p in range(PAIRS):
            d = D[p]
            h1 = d["g1"] * d["slope"]
            h1b = h1.astype(bf16)
            w1n = w1s[p] - mm_tn(d["kmb"], h1b)
            db = jnp.concatenate([jnp.sum(h1[:64], axis=0, keepdims=True), jnp.sum(h1[64:], axis=0, keepdims=True)], axis=0)
            b1n = d["b1"] - db
            if m == 1:
                w1n = w1n.astype(bf16).astype(f32); b1n = b1n.astype(bf16).astype(f32)
            w1s[p] = w1n; b1s[p] = b1n
            d["h1b"] = h1b
        yield
        for p in range(PAIRS):
            d = D[p]
            qm_s[m, p, :, :128] = two(d["q"])
            qm_s[m, p, :, 128:] = d["m1"]
            wh_s[m, p, :128] = d["w1"]
            wh_s[m, p, 128:] = d["h1b"]
            wx_s[m, p, :128] = d["w2"]
            wx_s[m, p, 128:] = d["x2"]
            h2_s[m, p] = d["h2b"]
            b1_s[m, p] = d["b1"]
            b2_s[m, p] = d["b2"]
            q_s[m, p] = d["q"]
        yield

    def query(m, start):
        D = [dict() for _ in range(PAIRS)]
        for p in range(PAIRS):
            b1 = b1_s[m, p]
            bias = jnp.concatenate([jnp.broadcast_to(b1[0:1], (64, 256)), jnp.broadcast_to(b1[1:2], (64, 256))], axis=0)
            D[p]["zq"] = mm(qm_s[m, p], wh_s[m, p]) + bias
        yield
        for p in range(PAIRS):
            d = D[p]
            zq = d["zq"]
            xq = (zq * gate(zq)).astype(bf16)
            both = mm_nt(xq, wx_s[m, p])
            d["bw"] = both[:, :128]
            d["bx"] = both[:, 128:]
        yield
        for p in range(PAIRS):
            d = D[p]
            m2 = jnp.where(tri, one(d["bx"]) + 1.0, 0.0).astype(bf16)
            d["mh"] = mm(m2, h2_s[m, p])
        yield
        for p in range(PAIRS):
            d = D[p]
            y = q_s[m, p].astype(f32) + (one(d["bw"]) + b2_s[m, p]) - d["mh"]
            yy = y * y
            lo = jnp.sum(jnp.where(low, yy, 0.0), axis=1, keepdims=True)
            hi = jnp.sum(jnp.where(low, 0.0, yy), axis=1, keepdims=True)
            y = y * lax.rsqrt(jnp.where(low, lo, hi) * (1.0 / 64.0) + 1e-6)
            y = y * gain_ref[0:1, p * 128 : (p + 1) * 128]
            out_ref[pl.ds(start, MB), p * 128 : (p + 1) * 128] = y.astype(bf16)
        yield

    def weave(*gens):
        gens = list(gens)
        while gens:
            for g in list(gens):
                if next(g, "end") == "end":
                    gens.remove(g)

    before = pl.multiple_of(jnp.maximum(slab * 128 - MB, 0), MB)
    weave(train(0), query(1, before))
    weave(train(1), query(0, pl.multiple_of(slab * 128, MB)))

    @pl.when(slab == 7)
    def _():
        weave(query(1, pl.multiple_of(slab * 128 + MB, MB)))


def layer(place, tokens, weights, rate_t, rate_bias, init_weights, hidden, outer, gain):
    def whole(shape):
        return pl.BlockSpec(shape, lambda i, place: (0,) * len(shape))

    far = pl.BlockSpec(memory_space=pltpu.HBM)
    anywhere = pl.BlockSpec(memory_space=pl.ANY)
    pieces = len(TOKEN_PIECES) + len(WEIGHT_PIECES)
    return pl.pallas_call(
        layer_kernel,
        out_shape=jax.ShapeDtypeStruct((1024, 384), bf16),
        grid_spec=pltpu.PrefetchScalarGridSpec(
            num_scalar_prefetch=1,
            grid=(8,),
            in_specs=[far] * (NT + 1)
            + [anywhere]
            + [
                whole((24, 3072)),
                pl.BlockSpec(memory_space=pltpu.SMEM),
                pl.BlockSpec((2, 6, 64, 256), lambda i, place: (0, place[0], 0, 0)),
                whole((24, 256)),
                whole((24, 64)),
                pl.BlockSpec((1, 384), lambda i, place: (0, place[0])),
            ],
            out_specs=whole((1024, 384)),
            scratch_shapes=[
                pltpu.VMEM((PAIRS, 128, 256), f32),
                pltpu.VMEM((PAIRS, 128, 256), f32),
                pltpu.VMEM((PAIRS, 2, 256), f32),
                pltpu.VMEM((PAIRS, 1, 128), f32),
                pltpu.VMEM((2, PAIRS, 128, 256), bf16),
                pltpu.VMEM((2, PAIRS, 256, 256), bf16),
                pltpu.VMEM((2, PAIRS, 256, 256), bf16),
                pltpu.VMEM((2, PAIRS, 128, 128), bf16),
                pltpu.VMEM((2, PAIRS, 2, 256), f32),
                pltpu.VMEM((2, PAIRS, 1, 128), f32),
                pltpu.VMEM((2, PAIRS, 64, 128), bf16),
                pltpu.VMEM((1024, 3072), bf16),
                pltpu.VMEM((3072, 1280), bf16),
                pltpu.VMEM((1024, 1152), bf16),
                pltpu.VMEM((1024, 128), f32),
                pltpu.SemaphoreType.DMA((pieces,)),
            ],
        ),
        compiler_params=pltpu.CompilerParams(
            dimension_semantics=("arbitrary",), vmem_limit_bytes=60 << 20
        ),
        name="layer",
    )(place, *tokens, *weights, rate_t, rate_bias, init_weights, hidden, outer, gain)


DP = ("yl", "z", "c")
SEQ = ("x", "yh")
swap = [(0, 1), (1, 0)]


def ring(size, step):
    return [(i, (i + step) % size) for i in range(size)]


def after(value, others):
    return lax.optimization_barrier((value, others))[0]


def on_device(
    frames,
    proj_weight,
    rate_weight,
    rate_bias,
    init_weights,
    init_bias_hidden,
    init_bias_out,
    out_gain,
):
    x, yh, yl, z, c = (lax.axis_index(name) for name in ("x", "yh", "yl", "z", "c"))

    up, down = ring(4, 1), ring(4, -1)

    part = jnp.concatenate(
        [lax.dynamic_slice(proj_weight, (0, i * 1536 + x * 384), (96, 384)) for i in range(3)], axis=1
    )
    mine = lax.dynamic_index_in_dim(frames, yh, 0, keepdims=False)
    sent = lax.dynamic_index_in_dim(frames, 1 - yh, 0, keepdims=False)
    theirs = lax.ppermute(sent, "yh", swap)
    a1, b1 = lax.ppermute(mine, "x", up), lax.ppermute(mine, "x", down)
    t0, t1, a1, b1 = lax.optimization_barrier((theirs[:64], theirs[64:], a1, b1))
    a2, b2 = lax.ppermute(t0, "x", up), lax.ppermute(t1, "x", down)
    a3, b3 = jnp.concatenate([a1[:64], t1]), jnp.concatenate([b1[64:], t0])
    a3, b3, a2, b2 = lax.optimization_barrier((a3, b3, a2, b2))
    a3, b3 = lax.ppermute(a3, "x", up), lax.ppermute(b3, "x", down)
    a4, b4 = lax.ppermute(a2, "x", up), lax.ppermute(b2, "x", down)
    tokens = [mine, a1, b1, a3, b3, theirs, a2, b2, a4, b4]
    pair = jnp.concatenate([part, lax.ppermute(part, "yl", swap)])
    gathered = lax.all_gather(pair, "z", axis=0, tiled=True)
    gathered = after(gathered, (a2, b2, a3, b3))
    weights = [gathered, lax.ppermute(gathered, "c", swap)]

    result = layer(
        jnp.stack([x, yh, yl, z, c]).astype(jnp.int32), tokens, weights, rate_weight.T, rate_bias,
        init_weights, init_bias_hidden, init_bias_out, out_gain.reshape(1, 1536),
    )
    result = lax.all_to_all(result.reshape(8, 128, 384), SEQ, 0, 0, tiled=True)
    result = result.reshape(4, 2, 128, 384)
    return jnp.concatenate([result[i] for i in range(4)], axis=2)


def solution(mesh):
    fine = Mesh(mesh.devices.reshape(4, 2, 2, 8, 2), ("x", "yh", "yl", "z", "c"))
    return jax.shard_map(
        on_device,
        mesh=fine,
        in_specs=(P(DP, SEQ, None), P(DP, None), P(), P(), P(), P(), P(), P()),
        out_specs=P(DP, SEQ, None),
        check_vma=False,
    )
```
